256 devices in a mesh: dp: 32 (over x, y, z_lo), cent: 8 (over z_hi, core).
Axes of the slice: x: 4, y: 4, z: 8 (z_hi: 4, z_lo: 2; z = z_hi * 2 + z_lo), core: 2. Of those that a mesh axis runs over, the one named last changes fastest.
Arguments:
- points: bfloat16 [32768, 256], P('dp'), may hold values from -8 to 8
- centroids: bfloat16 [32768, 256], P('cent'), may hold values from -0.5 to 0.5
Outputs:
- new_centroids: float32 [32768, 256], P('cent')
- counts: float32 [32768], P('cent')
- log_evidence: float32 [32768], P('dp')
The draws below stay inside these ranges and needn't reach their ends.
All inputs are finite; a program needn't handle non-finite values.
Results may differ from the reference program's by a relative error of at most 0.0016.
Values sent between devices are 32-bit elements; how exact they have to be, the bound alone decides.
A program may use at most 64 MiB of HBM per device.

```python
import math
import jax
import jax.numpy as jnp
from jax import lax

D = 256
CENTROIDS = 32768
TOTAL_ROWS = 32768


def aligned_signs(key):
    signs = jax.random.bernoulli(jax.random.fold_in(key, 7001), 0.5, (D,))
    return jnp.where(signs, 1.0, -1.0).astype(jnp.float32)


def draw_points(key, part):
    first = jax.random.fold_in(key, 11)
    base = jax.random.truncated_normal(first, -6.0, 6.0, (TOTAL_ROWS, D))
    index = jnp.arange(TOTAL_ROWS)
    strength = jnp.array([5.0, 6.0, 8.0], jnp.float32)[index // 251 % 3]
    chosen = index % 251 == 7
    signs = aligned_signs(key)
    base = jnp.where(chosen[:, None], strength[:, None] * signs[None, :], base)
    return base.astype(jnp.float32).astype(jnp.bfloat16)


def draw_centroids(key, part):
    first = jax.random.fold_in(key, 21)
    base = jax.random.truncated_normal(first, -6.0, 6.0, (CENTROIDS, D)) / 16.0
    index = jnp.arange(CENTROIDS)
    signs = aligned_signs(key)
    leading = jnp.arange(D) == 0
    second = jnp.where(leading, 0.375, 0.5) * signs
    base = jnp.where((index % 509 == 5)[:, None], 0.5 * signs[None, :], base)
    base = jnp.where((index % 509 == 6)[:, None], second[None, :], base)
    return base.astype(jnp.float32).astype(jnp.bfloat16)


def setup_inputs(seed: int = 0) -> dict:
    key_of = jax.random.split(jax.random.key(seed), 3)
    points = draw_points(jax.random.fold_in(key_of[2], 71), 0)
    centroids = draw_centroids(jax.random.fold_in(key_of[2], 71), 0)
    return dict(points=points, centroids=centroids)


prior_mass = 0.5


def reference(points, centroids):
    cnorm = jnp.einsum("kd,kd->k", centroids, centroids, preferred_element_type=jnp.float32)
    block = min(512, TOTAL_ROWS)
    pieces = points.reshape(TOTAL_ROWS // block, block, D)

    def visit(carry, piece):
        sums, counts = carry
        score = 2.0 * jnp.dot(piece, centroids.T, preferred_element_type=jnp.float32) - cnorm[None, :]
        top = jnp.max(score, axis=1)
        weights = jnp.exp(score - top[:, None])
        total = jnp.sum(weights, axis=1)
        resp = (weights / total[:, None]).astype(jnp.bfloat16)
        sums = sums + jnp.dot(resp.T, piece, preferred_element_type=jnp.float32)
        counts = counts + jnp.sum(resp.astype(jnp.float32), axis=0)
        return (sums, counts), top + jnp.log(total) - math.log(CENTROIDS)

    start = (jnp.zeros((CENTROIDS, D), jnp.float32), jnp.zeros((CENTROIDS,), jnp.float32))
    (sums, counts), evidence = lax.scan(visit, start, pieces)
    new_centroids = (sums + prior_mass * centroids.astype(jnp.float32)) / (counts + prior_mass)[:, None]
    return new_centroids, counts, evidence.reshape(TOTAL_ROWS)
```

```python
import functools
import math

import jax
import jax.numpy as jnp
from jax import lax
from jax.experimental import pallas as pl
from jax.experimental.pallas import tpu as pltpu
from jax.sharding import PartitionSpec as P

MESH = pl.DeviceIdType.MESH
prior_mass = 0.5

NX, NY, NZ = 4, 4, 2
BLOCKS = 4
TILE = 256
F32, BF16 = jnp.float32, jnp.bfloat16

ORDER = None


def stage_order(blocks, stages):
    order = [(0, 0), (1, 0)]
    step = 2
    for tau in range(1, stages + step * blocks):
        for s in range(blocks):
            stage = tau - step * s
            if s >= 1:
                stage = tau - step * (s - 1) - 1
            if 0 <= stage < stages and (s, stage) not in order:
                order.append((s, stage))
    return order


def kernel(sizes, x_ref, c_ref, sum_ref, count_ref, log_ref,
           xt, xs, et, cb, part, rxu, rxv, rxz, soft, q, qr,
           soft_send, soft_recv, q_send, q_recv, send, recv):
    rows, cents, width, groups = sizes
    every_centroid = cents * groups
    dp, cent = lax.axis_index("dp"), lax.axis_index("cent")
    px, py, pz = dp // (NY * NZ), (dp // NZ) % NY, dp % NZ

    def at(x=None, y=None, z=None):
        x = px if x is None else x
        y = py if y is None else y
        z = pz if z is None else z
        return {"dp": (x * NY + y) * NZ + z, "cent": cent}

    def along(axis, offset):
        if axis == 0:
            return at(x=(px + offset) % NX)
        return at(y=(py + offset) % NY)

    partners = [along(a, d) for a in (0, 1) for d in (1, 2, 3)] + [at(z=1 - pz)]
    partners += [{"dp": dp, "cent": (cent + d) % groups} for d in range(1, groups)]
    barrier = pltpu.get_barrier_semaphore()
    for device in partners:
        pl.semaphore_signal(barrier, inc=1, device_id=device, device_id_type=MESH)

    xt[...] = jnp.transpose(x_ref[...].astype(F32) * 2.0).astype(BF16)

    def largest(b, top):
        at_rows = pl.ds(pl.multiple_of(b * TILE, TILE), TILE)
        c = c_ref[at_rows, :]
        cf = c.astype(F32)
        norm = jnp.sum(cf * cf, axis=1, keepdims=True)
        cb[at_rows, :] = jnp.broadcast_to(norm, (TILE, 128))
        dots = jnp.dot(c, xt[...], preferred_element_type=F32)
        score = dots - norm
        return jnp.maximum(top, jnp.max(score.reshape(TILE // 8, 8, rows), axis=0))

    top8 = lax.fori_loop(0, cents // TILE, largest, jnp.full((8, rows), -jnp.inf, F32))
    top1 = jnp.max(top8, axis=0, keepdims=True)

    def weigh(b, total):
        at_rows = pl.ds(pl.multiple_of(b * TILE, TILE), TILE)
        dots = jnp.dot(c_ref[at_rows, :], xt[...], preferred_element_type=F32)
        norm = cb[at_rows, 0:1]
        e = jnp.exp((dots - norm) - top1)
        et[at_rows, :] = e.astype(BF16)
        return total + jnp.sum(e.reshape(TILE // 8, 8, rows), axis=0)

    total8 = lax.fori_loop(0, cents // TILE, weigh, jnp.zeros((8, rows), F32))
    total1 = jnp.sum(total8, axis=0, keepdims=True)

    lanes = rows // 8
    soft[cent, 0:8, :] = jnp.concatenate([top1[:, i * lanes:(i + 1) * lanes] for i in range(8)], axis=0)
    soft[cent, 8:16, :] = jnp.concatenate([total1[:, i * lanes:(i + 1) * lanes] for i in range(8)], axis=0)

    pl.semaphore_wait(barrier, len(partners))

    def soft_copy(slot, device):
        return pltpu.make_async_remote_copy(
            src_ref=soft.at[slot], dst_ref=soft.at[slot], send_sem=soft_send.at[slot], recv_sem=soft_recv.at[slot],
            device_id=device, device_id_type=MESH)

    soft_out = []
    for d in range(1, groups):
        peer = (cent + d) % groups
        copy = pltpu.make_async_remote_copy(
            src_ref=soft.at[cent], dst_ref=soft.at[cent], send_sem=soft_send.at[d], recv_sem=soft_recv.at[cent],
            device_id={"dp": dp, "cent": peer}, device_id_type=MESH)
        copy.start()
        soft_out.append(copy)
    for d in range(1, groups):
        peer = (cent + d) % groups
        soft_copy(peer, {"dp": dp, "cent": peer}).wait_recv()
    tops = [soft[g, 0:8, :] for g in range(groups)]
    top = functools.reduce(jnp.maximum, tops)
    total = jnp.zeros_like(top)
    for g in range(groups):
        total = total + soft[g, 8:16, :] * jnp.exp(tops[g] - top)
    log_ref[...] = top + jnp.log(total) - math.log(every_centroid)
    scale = jnp.exp(soft[cent, 0:8, :] - top) / total

    for i in range(8):
        column = jnp.transpose(jnp.broadcast_to(scale[i:i + 1, :], (lanes, lanes)))
        at_rows = slice(i * lanes, (i + 1) * lanes)
        x = x_ref[at_rows, :].astype(F32)
        xs[at_rows, 0:width] = jnp.concatenate(
            [(x[:, j:j + lanes] * column).astype(BF16) for j in range(0, width, lanes)], axis=1)
        high = column.astype(BF16)
        low = (column - high.astype(F32)).astype(BF16)
        lane = lax.broadcasted_iota(jnp.int32, (lanes, lanes), 1)
        xs[at_rows, width:width + lanes] = jnp.where(lane < lanes // 2, high.astype(F32), low.astype(F32)).astype(BF16)

    block_rows = cents // (2 * BLOCKS)
    urows, vrows = block_rows // 4, block_rows // 16
    zrows = vrows // 2

    eye = (lax.broadcasted_iota(jnp.int32, (128, 128), 0) == lax.broadcasted_iota(jnp.int32, (128, 128), 1))

    def sums(b, carry):
        start = pl.multiple_of(b * TILE, TILE)
        out = jnp.dot(et[pl.ds(start, TILE), :], xs[...], preferred_element_type=F32)
        part[pl.ds(start, TILE), :] = out[:, 0:width]
        c = out[:, width:width + 128]
        c = c + pltpu.roll(c, 64, 1)
        for i in range(TILE // 128):
            row = jnp.sum(jnp.where(eye, c[i * 128:(i + 1) * 128, :], 0.0), axis=0, keepdims=True)
            q[pl.ds(b * (TILE // 128) + i, 1), :] = row
        return carry

    started = []

    def remote(src, dst, k, device):
        return pltpu.make_async_remote_copy(
            src_ref=src, dst_ref=dst, send_sem=send.at[k], recv_sem=recv.at[k], device_id=device, device_id_type=MESH)

    def go(src, dst, k, device):
        copy = remote(src, dst, k, device)
        copy.start()
        started.append(copy)

    def arrived(dst, k):
        remote(dst, dst, k, at(z=1 - pz)).wait_recv()

    def rows_of(ref, start, size):
        return ref.at[pl.ds(pl.multiple_of(start, 8), size), :]

    def add(start, size, *others):
        here = pl.ds(pl.multiple_of(start, 8), size)
        value = part[here, :]
        for other in others:
            value = value + other[...]
        part[here, :] = value

    per = 22

    def ring_first(block, k, axis, position, base, size, rx):
        half = size // 2
        plus, minus = along(axis, 1), along(axis, 3)
        opposite, after, before = [base + ((position + d) % 4) * size for d in (2, 1, 3)]
        go(rows_of(part, opposite, half), rx.at[block, 0], k, plus)
        go(rows_of(part, opposite + half, half), rx.at[block, 1], k + 1, minus)
        go(rows_of(part, after + half, half), rx.at[block, 2], k + 2, plus)
        go(rows_of(part, before, half), rx.at[block, 3], k + 3, minus)

    def ring_second(block, k, axis, position, base, size, rx):
        half = size // 2
        plus, minus = along(axis, 1), along(axis, 3)
        after, before = [base + ((position + d) % 4) * size for d in (1, 3)]
        arrived(rx.at[block, 0], k)
        add(after, half, rx.at[block, 0])
        go(rows_of(part, after, half), rx.at[block, 4], k + 4, plus)
        arrived(rx.at[block, 1], k + 1)
        add(before + half, half, rx.at[block, 1])
        go(rows_of(part, before + half, half), rx.at[block, 5], k + 5, minus)

    def ring_third(block, k, position, base, size, rx):
        half = size // 2
        mine = base + position * size
        arrived(rx.at[block, 2], k + 2)
        arrived(rx.at[block, 3], k + 3)
        arrived(rx.at[block, 4], k + 4)
        add(mine, half, rx.at[block, 3], rx.at[block, 4])
        arrived(rx.at[block, 5], k + 5)
        add(mine + half, half, rx.at[block, 2], rx.at[block, 5])

    def spread_first(k, axis, position, base, size):
        mine = rows_of(sum_ref, base + position * size, size)
        go(mine, mine, k, along(axis, 1))
        go(mine, mine, k + 1, along(axis, 3))

    def spread_second(k, axis, position, base, size):
        half = size // 2
        before, after = [base + ((position + d) % 4) * size for d in (3, 1)]
        arrived(rows_of(sum_ref, before, size), k)
        there = rows_of(sum_ref, before, half)
        go(there, there, k + 2, along(axis, 1))
        arrived(rows_of(sum_ref, after, size), k + 1)
        there = rows_of(sum_ref, after + half, half)
        go(there, there, k + 3, along(axis, 3))

    def spread_third(k, position, base, size):
        half = size // 2
        opposite = base + ((position + 2) % 4) * size
        arrived(rows_of(sum_ref, opposite, half), k + 2)
        arrived(rows_of(sum_ref, opposite + half, half), k + 3)

    STAGES = 11

    def stage(h, s, number):
        block = h * BLOCKS + s
        base = block * block_rows
        k = block * per
        uaxis, vaxis = (0, 1) if h == 0 else (1, 0)
        u, v = (px, py) if h == 0 else (py, px)
        chunk = base + u * urows
        piece = chunk + v * vrows
        own, other = piece + pz * zrows, piece + (1 - pz) * zrows
        if number == 0:
            lax.fori_loop(base // TILE, (base + block_rows) // TILE, sums, 0)
            ring_first(block, k, uaxis, u, base, urows, rxu)
        elif number == 1:
            ring_second(block, k, uaxis, u, base, urows, rxu)
        elif number == 2:
            ring_third(block, k, u, base, urows, rxu)
            ring_first(block, k + 6, vaxis, v, chunk, vrows, rxv)
        elif number == 3:
            ring_second(block, k + 6, vaxis, v, chunk, vrows, rxv)
        elif number == 4:
            ring_third(block, k + 6, v, chunk, vrows, rxv)
            go(rows_of(part, other, zrows), rxz.at[block], k + 12, at(z=1 - pz))
        elif number == 5:
            arrived(rxz.at[block], k + 12)
            here = pl.ds(pl.multiple_of(own, 8), zrows)
            sum_ref[here, :] = part[here, :] + rxz[block]
            go(rows_of(sum_ref, own, zrows), rows_of(sum_ref, own, zrows), k + 13, at(z=1 - pz))
        elif number == 6:
            arrived(rows_of(sum_ref, other, zrows), k + 13)
            spread_first(k + 14, vaxis, v, chunk, vrows)
        elif number == 7:
            spread_second(k + 14, vaxis, v, chunk, vrows)
        elif number == 8:
            spread_third(k + 14, v, chunk, vrows)
            spread_first(k + 18, uaxis, u, base, urows)
        elif number == 9:
            spread_second(k + 18, uaxis, u, base, urows)
        elif number == 10:
            spread_third(k + 18, u, base, urows)

    def count_copy(level, source, k, device, slot):
        return pltpu.make_async_remote_copy(
            src_ref=source, dst_ref=qr.at[level, slot], send_sem=q_send.at[k], recv_sem=q_recv.at[level, slot],
            device_id=device, device_id_type=MESH)

    def counts_send(level):
        position = (px, py, pz)[level]
        qr[level, position] = q[...]
        for d in range(1, (NX, NY, NZ)[level]):
            device = along(level, d) if level < 2 else at(z=1 - pz)
            copy = count_copy(level, qr.at[level, position], level * 3 + d - 1, device, position)
            copy.start()
            started.append(copy)

    def counts_take(level):
        position, size = (px, py, pz)[level], (NX, NY, NZ)[level]
        for d in range(1, size):
            slot = (position + d) % size
            count_copy(level, qr.at[level, slot], level * 3, at(z=1 - pz), slot).wait_recv()
        value = qr[level, 0]
        for i in range(1, size):
            value = value + qr[level, i]
        if level < 2:
            q[...] = value
        else:
            count_ref[...] = value

    done = 0
    for s, number in stage_order(BLOCKS, STAGES):
        for h in (0, 1):
            stage(h, s, number)
        if number == 0:
            done += 1
            if done == BLOCKS:
                counts_send(0)
        if s == BLOCKS - 1 and number == 2:
            counts_take(0)
            counts_send(1)
        if s == BLOCKS - 1 and number == 4:
            counts_take(1)
            counts_send(2)
        if s == BLOCKS - 1 and number == 6:
            counts_take(2)
    for copy in soft_out + started:
        copy.wait_send()


def body(points, centroids):
    rows, width = points.shape
    cents = centroids.shape[0]
    groups = lax.axis_size("cent")
    block_rows = cents // (2 * BLOCKS)
    urows, vrows = block_rows // 4, block_rows // 16
    vmem = pl.BlockSpec(memory_space=pltpu.VMEM)
    messages = 2 * BLOCKS * 22
    sums, counts, log_evidence = pl.pallas_call(
        functools.partial(kernel, (rows, cents, width, groups)),
        out_shape=(
            jax.ShapeDtypeStruct((cents, width), F32),
            jax.ShapeDtypeStruct((cents // 128, 128), F32),
            jax.ShapeDtypeStruct((8, rows // 8), F32),
        ),
        in_specs=[vmem] * 2,
        out_specs=(vmem,) * 3,
        scratch_shapes=[
            pltpu.VMEM((width, rows), BF16),
            pltpu.VMEM((rows, width + 128), BF16),
            pltpu.VMEM((cents, rows), BF16),
            pltpu.VMEM((cents, 128), F32),
            pltpu.VMEM((cents, width), F32),
            pltpu.VMEM((2 * BLOCKS, 6, urows // 2, width), F32),
            pltpu.VMEM((2 * BLOCKS, 6, vrows // 2, width), F32),
            pltpu.VMEM((2 * BLOCKS, vrows // 2, width), F32),
            pltpu.VMEM((groups, 16, rows // 8), F32),
            pltpu.VMEM((cents // 128, 128), F32),
            pltpu.VMEM((3, 4, cents // 128, 128), F32),
            pltpu.SemaphoreType.DMA((groups,)),
            pltpu.SemaphoreType.DMA((groups,)),
            pltpu.SemaphoreType.DMA((9,)),
            pltpu.SemaphoreType.DMA((3, 4)),
            pltpu.SemaphoreType.DMA((messages,)),
            pltpu.SemaphoreType.DMA((messages,)),
        ],
        compiler_params=pltpu.CompilerParams(
            collective_id=0, has_side_effects=True, vmem_limit_bytes=58 * 1024 * 1024),
    )(points, centroids)
    counts = counts.reshape(cents)
    new_centroids = (sums + prior_mass * centroids.astype(F32)) / (counts + prior_mass)[:, None]
    return new_centroids, counts, log_evidence.reshape(rows)


def solution(mesh):
    return jax.shard_map(
        body,
        mesh=mesh,
        in_specs=(P("dp", None), P("cent", None)),
        out_specs=(P("cent", None), P("cent"), P("dp")),
        check_vma=False,
    )
```

```python
import functools
import math

import jax
import jax.numpy as jnp
from jax import lax
from jax.experimental import pallas as pl
from jax.experimental.pallas import tpu as pltpu
from jax.sharding import PartitionSpec as P

MESH = pl.DeviceIdType.MESH
prior_mass = 0.5

NX, NY, NZ = 4, 4, 2
TILE = 512
F32, BF16 = jnp.float32, jnp.bfloat16

BLOCKS = (
    (512, 0, True),
    (512, 1, True),
    (512, 0, False),
    (512, 1, False),
    (1024, 0, False),
    (1024, 1, False),
)
ORDER = (
    2, 1, 5, 0, 4, 3, 6, 2, 5, 4, 1, 3, 6, 2, 0, 5, 1, 4, 3, 0, 6, 2, 5, 1, 4, 3, 0, 6, 2, 5, 1, 4, 3, 0, 2, 1, 5, 4,
    3, 0, 2, 1, 5, 4, 0, 3, 2, 1, 5, 3, 4, 0, 2, 1, 5, 3, 4, 0, 1, 2, 5, 1, 4, 0, 3, 2, 5, 0, 3, 4,
)


def programs(o, px, py, pz):
    result = []
    base = 0
    for index, (rows, h, zfirst) in enumerate(BLOCKS):
        result.append(block_program(o, index, base, rows, h, zfirst, px, py, pz))
        base += rows
    result.append(count_program(o))
    return result


def block_program(o, index, base, rows, h, zfirst, px, py, pz):
    names = (("x+", "x-"), ("y+", "y-"))
    udir, vdir = names[h], names[1 - h]
    u, v = ((px, py), (py, px))[h]
    ubase = base + pz * (rows // 2) if zfirst else base
    span = rows // 2 if zfirst else rows
    urows, vrows = span // 4, span // 16
    zrows = vrows // 2
    chunk = ubase + u * urows
    piece = chunk + v * vrows
    own, other = piece + pz * zrows, piece + (1 - pz) * zrows

    def key(tag, level):
        return (index, tag, level)

    def first(level, d, p, start, size):
        half = size // 2
        opposite, after, before = [start + ((p + i) % 4) * size for i in (2, 1, 3)]
        o.send_part(d[0], opposite, half, key("o+", level))
        o.send_part(d[1], opposite + half, half, key("o-", level))
        o.send_part(d[0], after + half, half, key("d+", level))
        o.send_part(d[1], before, half, key("d-", level))

    def second(level, d, p, start, size):
        half = size // 2
        after, before = [start + ((p + i) % 4) * size for i in (1, 3)]
        o.wait(key("o+", level), half)
        o.add(after, half, [key("o+", level)])
        o.send_part(d[0], after, half, key("c+", level))
        o.wait(key("o-", level), half)
        o.add(before + half, half, [key("o-", level)])
        o.send_part(d[1], before + half, half, key("c-", level))

    def third(level, p, start, size, final=False):
        half = size // 2
        mine = start + p * size
        for tag in ("d+", "d-", "c+", "c-"):
            o.wait(key(tag, level), half)
        o.add(mine, half, [key("d-", level), key("c+", level)], final)
        o.add(mine + half, half, [key("d+", level), key("c-", level)], final)

    def spread_first(level, d, p, start, size):
        o.send_sum(d[0], start + p * size, size, key("f+", level))
        o.send_sum(d[1], start + p * size, size, key("f-", level))

    def spread_second(level, d, p, start, size):
        half = size // 2
        before, after = [start + ((p + i) % 4) * size for i in (3, 1)]
        o.wait_sum(key("f+", level), before, size)
        o.send_sum(d[0], before, half, key("g+", level))
        o.wait_sum(key("f-", level), after, size)
        o.send_sum(d[1], after + half, half, key("g-", level))

    def spread_third(level, p, start, size):
        half = size // 2
        opposite = start + ((p + 2) % 4) * size
        o.wait_sum(key("g+", level), opposite, half)
        o.wait_sum(key("g-", level), opposite + half, half)

    def zsend(n):
        place = ubase + ((u + n) % 4) * urows
        o.send_sum("z", place, urows, key("h", n))

    def zwait(n):
        place = base + (1 - pz) * (rows // 2) + ((u + n) % 4) * urows
        o.wait_sum(key("h", n), place, urows)

    if zfirst:
        def s0():
            o.sums(base, rows)
            o.send_part("z", base + (1 - pz) * span, span, key("z", 0))

        def s1():
            o.wait(key("z", 0), span)
            o.add(ubase, span, [key("z", 0)])
            first(0, udir, u, ubase, urows)

        def s5():
            third(1, v, chunk, vrows, True)
            spread_first(1, vdir, v, chunk, vrows)

        def s7():
            spread_third(1, v, chunk, vrows)
            spread_first(0, udir, u, ubase, urows)
            zsend(0)

        def s8():
            spread_second(0, udir, u, ubase, urows)
            zsend(1)
            zsend(3)

        def s9():
            spread_third(0, u, ubase, urows)
            zsend(2)

        return [
            s0, s1,
            lambda: second(0, udir, u, ubase, urows),
            lambda: (third(0, u, ubase, urows), first(1, vdir, v, chunk, vrows)),
            lambda: second(1, vdir, v, chunk, vrows),
            s5,
            lambda: spread_second(1, vdir, v, chunk, vrows),
            s7, s8, s9,
            lambda: [zwait(n) for n in range(4)],
        ]

    def t4():
        third(1, v, chunk, vrows)
        o.send_part("z", other, zrows, key("z", 0))

    def t5():
        o.wait(key("z", 0), zrows)
        o.add(own, zrows, [key("z", 0)], True)
        o.send_sum("z", own, zrows, key("h", 0))

    def t6():
        o.wait_sum(key("h", 0), other, zrows)
        spread_first(1, vdir, v, chunk, vrows)

    return [
        lambda: (o.sums(base, rows), first(0, udir, u, base, urows)),
        lambda: second(0, udir, u, base, urows),
        lambda: (third(0, u, base, urows), first(1, vdir, v, chunk, vrows)),
        lambda: second(1, vdir, v, chunk, vrows),
        t4, t5, t6,
        lambda: spread_second(1, vdir, v, chunk, vrows),
        lambda: (spread_third(1, v, chunk, vrows), spread_first(0, udir, u, base, urows)),
        lambda: spread_second(0, udir, u, base, urows),
        lambda: spread_third(0, u, base, urows),
    ]


def count_program(o):
    return [
        lambda: (o.counts(), o.count_send(0)),
        lambda: (o.count_take(0), o.count_send(1)),
        lambda: (o.count_take(1), o.count_send(2)),
        lambda: o.count_take(2),
    ]


class Messages:
    def __init__(self):
        self.ids, self.places, self.rows = {}, {}, 0

    def number(self, key):
        return self.ids.setdefault(key, len(self.ids))

    def send_part(self, direction, start, size, key):
        self.number(key)
        self.places[key] = (self.rows, size)
        self.rows += size

    def send_sum(self, direction, start, size, key):
        self.number(key)

    def wait(self, *_):
        pass

    wait_sum = add = sums = counts = count_send = count_take = wait


def messages():
    found = Messages()
    for stages in programs(found, 0, 0, 0):
        for run in stages:
            run()
    return found


def kernel(sizes, x_ref, c_ref, sum_ref, count_ref, log_ref,
           xt, xs, et, cb, part, rx, scales, soft, q, qr,
           soft_send, soft_recv, q_send, q_recv, send, recv):
    rows, cents, width, groups = sizes
    every_centroid = cents * groups
    dp, cent = lax.axis_index("dp"), lax.axis_index("cent")
    px, py, pz = dp // (NY * NZ), (dp // NZ) % NY, dp % NZ

    def at(x=None, y=None, z=None):
        x = px if x is None else x
        y = py if y is None else y
        z = pz if z is None else z
        return {"dp": (x * NY + y) * NZ + z, "cent": cent}

    def along(axis, offset):
        if axis == 0:
            return at(x=(px + offset) % NX)
        return at(y=(py + offset) % NY)

    partners = [along(a, d) for a in (0, 1) for d in (1, 2, 3)] + [at(z=1 - pz)]
    partners += [{"dp": dp, "cent": (cent + d) % groups} for d in range(1, groups)]
    barrier = pltpu.get_barrier_semaphore()
    for device in partners:
        pl.semaphore_signal(barrier, inc=1, device_id=device, device_id_type=MESH)

    xt[...] = jnp.transpose(x_ref[...].astype(F32) * 2.0).astype(BF16)

    def largest(b, top):
        at_rows = pl.ds(pl.multiple_of(b * TILE, TILE), TILE)
        c = c_ref[at_rows, :]
        cf = c.astype(F32)
        norm = jnp.sum(cf * cf, axis=1, keepdims=True)
        cb[at_rows, :] = jnp.broadcast_to(norm, (TILE, 128))
        dots = jnp.dot(c, xt[...], preferred_element_type=F32)
        score = dots - norm
        return jnp.maximum(top, jnp.max(score.reshape(TILE // 8, 8, rows), axis=0))

    top8 = lax.fori_loop(0, cents // TILE, largest, jnp.full((8, rows), -jnp.inf, F32))
    top1 = jnp.max(top8, axis=0, keepdims=True)

    def weigh(b, total):
        at_rows = pl.ds(pl.multiple_of(b * TILE, TILE), TILE)
        dots = jnp.dot(c_ref[at_rows, :], xt[...], preferred_element_type=F32)
        norm = cb[at_rows, 0:1]
        e = jnp.exp((dots - norm) - top1)
        et[at_rows, :] = e.astype(BF16)
        return total + jnp.sum(e.reshape(TILE // 8, 8, rows), axis=0)

    total8 = lax.fori_loop(0, cents // TILE, weigh, jnp.zeros((8, rows), F32))
    total1 = jnp.sum(total8, axis=0, keepdims=True)

    lanes = rows // 8
    soft[cent, 0:8, :] = jnp.concatenate([top1[:, i * lanes:(i + 1) * lanes] for i in range(8)], axis=0)
    soft[cent, 8:16, :] = jnp.concatenate([total1[:, i * lanes:(i + 1) * lanes] for i in range(8)], axis=0)

    pl.semaphore_wait(barrier, len(partners))

    def soft_copy(slot, device):
        return pltpu.make_async_remote_copy(
            src_ref=soft.at[slot], dst_ref=soft.at[slot], send_sem=soft_send.at[slot], recv_sem=soft_recv.at[slot],
            device_id=device, device_id_type=MESH)

    soft_out = []
    for d in range(1, groups):
        peer = (cent + d) % groups
        copy = pltpu.make_async_remote_copy(
            src_ref=soft.at[cent], dst_ref=soft.at[cent], send_sem=soft_send.at[d], recv_sem=soft_recv.at[cent],
            device_id={"dp": dp, "cent": peer}, device_id_type=MESH)
        copy.start()
        soft_out.append(copy)
    for d in range(1, groups):
        peer = (cent + d) % groups
        soft_copy(peer, {"dp": dp, "cent": peer}).wait_recv()
    tops = [soft[g, 0:8, :] for g in range(groups)]
    top = functools.reduce(jnp.maximum, tops)
    total = jnp.zeros_like(top)
    for g in range(groups):
        total = total + soft[g, 8:16, :] * jnp.exp(tops[g] - top)
    log_ref[...] = top + jnp.log(total) - math.log(every_centroid)
    scale = jnp.exp(soft[cent, 0:8, :] - top) / total

    for i in range(8):
        column = jnp.transpose(jnp.broadcast_to(scale[i:i + 1, :], (lanes, lanes)))
        at_rows = slice(i * lanes, (i + 1) * lanes)
        x = x_ref[at_rows, :].astype(F32)
        xs[at_rows, :] = jnp.concatenate(
            [(x[:, j:j + lanes] * column).astype(BF16) for j in range(0, width, lanes)], axis=1)
    high = scale.astype(BF16).astype(F32)
    low = scale - high
    filler = jnp.zeros((14, lanes), F32)
    for i in range(8):
        both = jnp.concatenate([high[i:i + 1, :], low[i:i + 1, :], filler], axis=0)
        scales[:, i * lanes:(i + 1) * lanes] = both.astype(BF16)

    started = []

    found = messages()

    def remote(src, dst, k, device):
        return pltpu.make_async_remote_copy(
            src_ref=src, dst_ref=dst, send_sem=send.at[k], recv_sem=recv.at[k], device_id=device, device_id_type=MESH)

    devices = {"x+": along(0, 1), "x-": along(0, 3), "y+": along(1, 1), "y-": along(1, 3), "z": at(z=1 - pz)}

    def rows_of(ref, start, size):
        return ref.at[pl.ds(start if isinstance(start, int) else pl.multiple_of(start, 8), size), :]

    class Issue:
        def sums(self, start, size):
            tile = min(size, TILE)
            for i in range(start, start + size, tile):
                part[i:i + tile, :] = jnp.dot(et[i:i + tile, :], xs[...], preferred_element_type=F32)

        def send_part(self, direction, start, size, key):
            copy = remote(rows_of(part, start, size), rows_of(rx, found.places[key][0], size), found.number(key), devices[direction])
            copy.start()
            started.append(copy)

        def send_sum(self, direction, start, size, key):
            here = rows_of(sum_ref, start, size)
            copy = remote(here, here, found.number(key), devices[direction])
            copy.start()
            started.append(copy)

        def wait(self, key, size):
            here = rows_of(rx, found.places[key][0], size)
            remote(here, here, found.number(key), devices["z"]).wait_recv()

        def wait_sum(self, key, start, size):
            here = rows_of(sum_ref, start, size)
            remote(here, here, found.number(key), devices["z"]).wait_recv()

        def add(self, start, size, keys, final=False):
            here = pl.ds(pl.multiple_of(start, 8), size)
            value = part[here, :]
            for key in keys:
                place = found.places[key][0]
                value = value + rx[place:place + size, :]
            if final:
                sum_ref[here, :] = value
            else:
                part[here, :] = value

        def counts(self):
            def one(b, carry):
                start = pl.multiple_of(b * TILE, TILE)
                out = lax.dot_general(scales[...], et[pl.ds(start, TILE), :], (((1,), (1,)), ((), ())),
                                      preferred_element_type=F32)
                row = out[0:1, :] + out[1:2, :]
                for i in range(TILE // 128):
                    q[pl.ds(b * (TILE // 128) + i, 1), :] = row[:, i * 128:(i + 1) * 128]
                return carry

            lax.fori_loop(0, cents // TILE, one, 0)

        def copy(self, level, source, k, device, slot):
            return pltpu.make_async_remote_copy(
                src_ref=source, dst_ref=qr.at[level, slot], send_sem=q_send.at[k], recv_sem=q_recv.at[level, slot],
                device_id=device, device_id_type=MESH)

        def count_send(self, level):
            position = (px, py, pz)[level]
            qr[level, position] = q[...]
            for d in range(1, (NX, NY, NZ)[level]):
                device = along(level, d) if level < 2 else at(z=1 - pz)
                copy = self.copy(level, qr.at[level, position], level * 3 + d - 1, device, position)
                copy.start()
                started.append(copy)

        def count_take(self, level):
            position, size = (px, py, pz)[level], (NX, NY, NZ)[level]
            for d in range(1, size):
                slot = (position + d) % size
                self.copy(level, qr.at[level, slot], level * 3, at(z=1 - pz), slot).wait_recv()
            value = qr[level, 0]
            for i in range(1, size):
                value = value + qr[level, i]
            if level < 2:
                q[...] = value
            else:
                count_ref[...] = value

    stages = [iter(p) for p in programs(Issue(), px, py, pz)]
    for block in ORDER:
        next(stages[block])()
    for copy in soft_out + started:
        copy.wait_send()


def body(points, centroids):
    rows, width = points.shape
    cents = centroids.shape[0]
    groups = lax.axis_size("cent")
    found = messages()
    vmem = pl.BlockSpec(memory_space=pltpu.VMEM)
    sums, counts, log_evidence = pl.pallas_call(
        functools.partial(kernel, (rows, cents, width, groups)),
        out_shape=(
            pltpu.VMEM((cents, width), F32),
            pltpu.VMEM((cents // 128, 128), F32),
            pltpu.VMEM((8, rows // 8), F32),
        ),
        in_specs=[vmem] * 2,
        out_specs=(vmem,) * 3,
        scratch_shapes=[
            pltpu.VMEM((width, rows), BF16),
            pltpu.VMEM((rows, width), BF16),
            pltpu.VMEM((cents, rows), BF16),
            pltpu.VMEM((cents, 128), F32),
            pltpu.VMEM((cents, width), F32),
            pltpu.VMEM((found.rows, width), F32),
            pltpu.VMEM((16, rows), BF16),
            pltpu.VMEM((groups, 16, rows // 8), F32),
            pltpu.VMEM((cents // 128, 128), F32),
            pltpu.VMEM((3, 4, cents // 128, 128), F32),
            pltpu.SemaphoreType.DMA((groups,)),
            pltpu.SemaphoreType.DMA((groups,)),
            pltpu.SemaphoreType.DMA((9,)),
            pltpu.SemaphoreType.DMA((3, 4)),
            pltpu.SemaphoreType.DMA((len(found.ids),)),
            pltpu.SemaphoreType.DMA((len(found.ids),)),
        ],
        compiler_params=pltpu.CompilerParams(
            collective_id=0, has_side_effects=True, vmem_limit_bytes=58 * 1024 * 1024),
    )(points, centroids)
    counts = counts.reshape(cents)
    new_centroids = (sums + prior_mass * centroids.astype(F32)) / (counts + prior_mass)[:, None]
    return new_centroids, counts, log_evidence.reshape(rows)


def solution(mesh):
    return jax.shard_map(
        body,
        mesh=mesh,
        in_specs=(P("dp", None), P("cent", None)),
        out_specs=(P("cent", None), P("cent"), P("dp")),
        check_vma=False,
    )
```

```python
import functools
import math

import jax
import jax.numpy as jnp
from jax import lax
from jax.experimental import pallas as pl
from jax.experimental.pallas import tpu as pltpu
from jax.sharding import PartitionSpec as P

MESH = pl.DeviceIdType.MESH
prior_mass = 0.5

NX, NY, NZ = 4, 4, 2
TILE = 512
LOAD = 1024
GROUP = 512
F32, BF16 = jnp.float32, jnp.bfloat16

BLOCKS = (
    (512, 0, True),
    (512, 1, True),
    (512, 0, False),
    (512, 1, False),
    (1024, 0, False),
    (1024, 1, False),
)
ORDER = (
    2, 3, 0, 4, 5, 3, 1, 4, 5, 2, 6, 0, 3, 4, 1, 5, 2, 0, 4, 1, 3, 5, 2, 4, 0, 3, 1, 6, 5, 2, 0, 4, 1, 3, 2, 5, 0, 1,
    4, 3, 0, 1, 5, 2, 3, 4, 0, 1, 2, 5, 3, 4, 6, 0, 2, 5, 6, 1, 4, 3, 0, 5, 1, 2, 0, 3, 4, 1, 5, 2,
)


def split(size):
    half = size // 16 * 8
    return half, size - half


def programs(o, px, py, pz):
    result = []
    base = 0
    for index, (rows, h, zfirst) in enumerate(BLOCKS):
        result.append(block_program(o, index, base, rows, h, zfirst, px, py, pz))
        base += rows
    result.append(count_program(o))
    return result


def block_program(o, index, base, rows, h, zfirst, px, py, pz):
    names = (("x+", "x-"), ("y+", "y-"))
    udir, vdir = names[h], names[1 - h]
    u, v = ((px, py), (py, px))[h]
    ubase = base + pz * (rows // 2) if zfirst else base
    span = rows // 2 if zfirst else rows
    urows, vrows = span // 4, span // 16
    zrows = vrows // 2
    chunk = ubase + u * urows
    piece = chunk + v * vrows
    own, other = piece + pz * zrows, piece + (1 - pz) * zrows

    def key(tag, level):
        return (index, tag, level)

    def first(level, d, p, start, size):
        half, rest = split(size)
        opposite, after, before = [start + ((p + i) % 4) * size for i in (2, 1, 3)]
        o.send_part(d[0], opposite, half, key("o+", level))
        o.send_part(d[1], opposite + half, rest, key("o-", level))
        o.send_part(d[0], after + half, rest, key("d+", level))
        o.send_part(d[1], before, half, key("d-", level))

    def second(level, d, p, start, size):
        half, rest = split(size)
        after, before = [start + ((p + i) % 4) * size for i in (1, 3)]
        o.wait(key("o+", level), half)
        o.add(after, half, [key("o+", level)])
        o.send_part(d[0], after, half, key("c+", level))
        o.wait(key("o-", level), rest)
        o.add(before + half, rest, [key("o-", level)])
        o.send_part(d[1], before + half, rest, key("c-", level))

    def third(level, p, start, size, final=False):
        half, rest = split(size)
        mine = start + p * size
        for tag, part in (("d+", rest), ("d-", half), ("c+", half), ("c-", rest)):
            o.wait(key(tag, level), part)
        o.add(mine, half, [key("d-", level), key("c+", level)], final)
        o.add(mine + half, rest, [key("d+", level), key("c-", level)], final)

    def spread_first(level, d, p, start, size):
        o.send_sum(d[0], start + p * size, size, key("f+", level))
        o.send_sum(d[1], start + p * size, size, key("f-", level))

    def spread_second(level, d, p, start, size):
        half, rest = split(size)
        before, after = [start + ((p + i) % 4) * size for i in (3, 1)]
        o.wait_sum(key("f+", level), before, size)
        o.send_sum(d[0], before, half, key("g+", level))
        o.wait_sum(key("f-", level), after, size)
        o.send_sum(d[1], after + half, rest, key("g-", level))

    def spread_third(level, p, start, size):
        half, rest = split(size)
        opposite = start + ((p + 2) % 4) * size
        o.wait_sum(key("g+", level), opposite, half)
        o.wait_sum(key("g-", level), opposite + half, rest)

    def zsend(n):
        place = ubase + ((u + n) % 4) * urows
        o.send_sum("z", place, urows, key("h", n))

    def zwait(n):
        place = base + (1 - pz) * (rows // 2) + ((u + n) % 4) * urows
        o.wait_sum(key("h", n), place, urows)

    if zfirst:
        def s0():
            o.sums(base, rows)
            o.send_part("z", base + (1 - pz) * span, span, key("z", 0))

        def s1():
            o.wait(key("z", 0), span)
            o.add(ubase, span, [key("z", 0)])
            first(0, udir, u, ubase, urows)

        def s5():
            third(1, v, chunk, vrows, True)
            spread_first(1, vdir, v, chunk, vrows)

        def s7():
            spread_third(1, v, chunk, vrows)
            spread_first(0, udir, u, ubase, urows)
            zsend(0)

        def s8():
            spread_second(0, udir, u, ubase, urows)
            zsend(1)
            zsend(3)

        def s9():
            spread_third(0, u, ubase, urows)
            zsend(2)

        return [
            s0, s1,
            lambda: second(0, udir, u, ubase, urows),
            lambda: (third(0, u, ubase, urows), first(1, vdir, v, chunk, vrows)),
            lambda: second(1, vdir, v, chunk, vrows),
            s5,
            lambda: spread_second(1, vdir, v, chunk, vrows),
            s7, s8, s9,
            lambda: ([zwait(n) for n in range(4)], o.norm(base, rows)),
        ]

    def t4():
        third(1, v, chunk, vrows)
        o.send_part("z", other, zrows, key("z", 0))

    def t5():
        o.wait(key("z", 0), zrows)
        o.add(own, zrows, [key("z", 0)], True)
        o.send_sum("z", own, zrows, key("h", 0))

    def t6():
        o.wait_sum(key("h", 0), other, zrows)
        spread_first(1, vdir, v, chunk, vrows)

    return [
        lambda: (o.sums(base, rows), first(0, udir, u, base, urows)),
        lambda: second(0, udir, u, base, urows),
        lambda: (third(0, u, base, urows), first(1, vdir, v, chunk, vrows)),
        lambda: second(1, vdir, v, chunk, vrows),
        t4, t5, t6,
        lambda: spread_second(1, vdir, v, chunk, vrows),
        lambda: (spread_third(1, v, chunk, vrows), spread_first(0, udir, u, base, urows)),
        lambda: spread_second(0, udir, u, base, urows),
        lambda: (spread_third(0, u, base, urows), o.norm(base, rows)),
    ]


def count_program(o):
    return [
        lambda: (o.counts(), o.count_send(0)),
        lambda: (o.count_take(0), o.count_send(1)),
        lambda: (o.count_take(1), o.count_send(2)),
        lambda: o.count_take(2),
    ]


class Messages:
    def __init__(self):
        self.ids, self.places, self.rows = {}, {}, 0

    def number(self, key):
        return self.ids.setdefault(key, len(self.ids))

    def send_part(self, direction, start, size, key):
        self.number(key)
        self.places[key] = (self.rows, size)
        self.rows += size

    def send_sum(self, direction, start, size, key):
        self.number(key)

    def wait(self, *_):
        pass

    wait_sum = add = norm = sums = counts = count_send = count_take = wait


def messages():
    found = Messages()
    for stages in programs(found, 0, 0, 0):
        for run in stages:
            run()
    return found


def kernel(sizes, x_ref, c_hbm, out_ref, count_ref, log_ref,
           c_ref, sum_ref, score, xt, xs, et, cb, part, rx, scales, soft, q, qr,
           c_sem, soft_send, soft_recv, q_send, q_recv, send, recv):
    rows, cents, width, groups = sizes
    every_centroid = cents * groups
    dp, cent = lax.axis_index("dp"), lax.axis_index("cent")
    px, py, pz = dp // (NY * NZ), (dp // NZ) % NY, dp % NZ

    def at(x=None, y=None, z=None):
        x = px if x is None else x
        y = py if y is None else y
        z = pz if z is None else z
        return {"dp": (x * NY + y) * NZ + z, "cent": cent}

    def along(axis, offset):
        if axis == 0:
            return at(x=(px + offset) % NX)
        return at(y=(py + offset) % NY)

    partners = [along(a, d) for a in (0, 1) for d in (1, 2, 3)] + [at(z=1 - pz)]
    partners += [{"dp": dp, "cent": (cent + d) % groups} for d in range(1, groups)]
    barrier = pltpu.get_barrier_semaphore()
    for device in partners:
        pl.semaphore_signal(barrier, inc=1, device_id=device, device_id_type=MESH)

    loads = []
    for i in range(cents // LOAD):
        here = slice(i * LOAD, (i + 1) * LOAD)
        loads.append(pltpu.make_async_copy(c_hbm.at[here, :], c_ref.at[here, :], c_sem.at[i]))
        loads[-1].start()

    xt[...] = jnp.transpose(x_ref[...].astype(F32) * 2.0).astype(BF16)

    tops, totals = [], []
    for g in range(rows // GROUP + 1):
        def visit(b, carry, g=g):
            top, total = carry
            here = pl.ds(pl.multiple_of(b * LOAD, LOAD), LOAD)
            if g < rows // GROUP:
                c = c_ref[here, :]
                if g == 0:
                    cf = c.astype(F32)
                    norm = jnp.sum(cf * cf, axis=1, keepdims=True)
                    cb[here, :] = jnp.broadcast_to(norm, (LOAD, 128))
                else:
                    norm = cb[here, 0:1]
                value = jnp.dot(c, xt[:, g * GROUP:(g + 1) * GROUP], preferred_element_type=F32) - norm
                score[g % 2, here, :] = value
                top = jnp.maximum(top, jnp.max(value.reshape(LOAD // 8, 8, GROUP), axis=0))
            if g > 0:
                e = jnp.exp(score[(g - 1) % 2, here, :] - tops[g - 1])
                et[here, (g - 1) * GROUP:g * GROUP] = e.astype(BF16)
                total = total + jnp.sum(e.reshape(LOAD // 8, 8, GROUP), axis=0)
            return top, total

        carry = (jnp.full((8, GROUP), -jnp.inf, F32), jnp.zeros((8, GROUP), F32))
        if g == 0:
            for b in range(cents // LOAD):
                loads[b].wait()
                carry = visit(b, carry)
        else:
            carry = lax.fori_loop(0, cents // LOAD, visit, carry)
        if g < rows // GROUP:
            tops.append(jnp.max(carry[0], axis=0, keepdims=True))
        if g > 0:
            totals.append(jnp.sum(carry[1], axis=0, keepdims=True))
    top1, total1 = jnp.concatenate(tops, axis=1), jnp.concatenate(totals, axis=1)

    lanes = rows // 8
    soft[cent, 0:8, :] = jnp.concatenate([top1[:, i * lanes:(i + 1) * lanes] for i in range(8)], axis=0)
    soft[cent, 8:16, :] = jnp.concatenate([total1[:, i * lanes:(i + 1) * lanes] for i in range(8)], axis=0)

    pl.semaphore_wait(barrier, len(partners))

    def soft_copy(slot, device):
        return pltpu.make_async_remote_copy(
            src_ref=soft.at[slot], dst_ref=soft.at[slot], send_sem=soft_send.at[slot], recv_sem=soft_recv.at[slot],
            device_id=device, device_id_type=MESH)

    soft_out = []
    for d in range(1, groups):
        peer = (cent + d) % groups
        copy = pltpu.make_async_remote_copy(
            src_ref=soft.at[cent], dst_ref=soft.at[cent], send_sem=soft_send.at[d], recv_sem=soft_recv.at[cent],
            device_id={"dp": dp, "cent": peer}, device_id_type=MESH)
        copy.start()
        soft_out.append(copy)
    for d in range(1, groups):
        peer = (cent + d) % groups
        soft_copy(peer, {"dp": dp, "cent": peer}).wait_recv()
    tops = [soft[g, 0:8, :] for g in range(groups)]
    top = functools.reduce(jnp.maximum, tops)
    total = jnp.zeros_like(top)
    for g in range(groups):
        total = total + soft[g, 8:16, :] * jnp.exp(tops[g] - top)
    log_ref[...] = top + jnp.log(total) - math.log(every_centroid)
    scale = jnp.exp(soft[cent, 0:8, :] - top) / total

    for i in range(8):
        column = jnp.transpose(jnp.broadcast_to(scale[i:i + 1, :], (lanes, lanes)))
        at_rows = slice(i * lanes, (i + 1) * lanes)
        x = x_ref[at_rows, :].astype(F32)
        xs[at_rows, :] = jnp.concatenate(
            [(x[:, j:j + lanes] * column).astype(BF16) for j in range(0, width, lanes)], axis=1)
    high = scale.astype(BF16).astype(F32)
    low = scale - high
    filler = jnp.zeros((14, lanes), F32)
    for i in range(8):
        both = jnp.concatenate([high[i:i + 1, :], low[i:i + 1, :], filler], axis=0)
        scales[:, i * lanes:(i + 1) * lanes] = both.astype(BF16)

    started = []

    found = messages()

    def remote(src, dst, k, device):
        return pltpu.make_async_remote_copy(
            src_ref=src, dst_ref=dst, send_sem=send.at[k], recv_sem=recv.at[k], device_id=device, device_id_type=MESH)

    devices = {"x+": along(0, 1), "x-": along(0, 3), "y+": along(1, 1), "y-": along(1, 3), "z": at(z=1 - pz)}

    def rows_of(ref, start, size):
        return ref.at[pl.ds(start if isinstance(start, int) else pl.multiple_of(start, 8), size), :]

    class Issue:
        def sums(self, start, size):
            tile = min(size, TILE)
            for i in range(start, start + size, tile):
                part[i:i + tile, :] = jnp.dot(et[i:i + tile, :], xs[...], preferred_element_type=F32)

        def send_part(self, direction, start, size, key):
            copy = remote(rows_of(part, start, size), rows_of(rx, found.places[key][0], size), found.number(key), devices[direction])
            copy.start()
            started.append(copy)

        def send_sum(self, direction, start, size, key):
            here = rows_of(sum_ref, start, size)
            copy = remote(here, here, found.number(key), devices[direction])
            copy.start()
            started.append(copy)

        def wait(self, key, size):
            here = rows_of(rx, found.places[key][0], size)
            remote(here, here, found.number(key), devices["z"]).wait_recv()

        def wait_sum(self, key, start, size):
            here = rows_of(sum_ref, start, size)
            remote(here, here, found.number(key), devices["z"]).wait_recv()

        def add(self, start, size, keys, final=False):
            here = pl.ds(pl.multiple_of(start, 8), size)
            value = part[here, :]
            for key in keys:
                place = found.places[key][0]
                value = value + rx[place:place + size, :]
            if final:
                sum_ref[here, :] = value
            else:
                part[here, :] = value

        def counts(self):
            def one(b, carry):
                start = pl.multiple_of(b * TILE, TILE)
                out = lax.dot_general(scales[...], et[pl.ds(start, TILE), :], (((1,), (1,)), ((), ())),
                                      preferred_element_type=F32)
                row = out[0:1, :] + out[1:2, :]
                for i in range(TILE // 128):
                    q[pl.ds(b * (TILE // 128) + i, 1), :] = row[:, i * 128:(i + 1) * 128]
                return carry

            lax.fori_loop(0, cents // TILE, one, 0)

        def copy(self, level, source, k, device, slot):
            return pltpu.make_async_remote_copy(
                src_ref=source, dst_ref=qr.at[level, slot], send_sem=q_send.at[k], recv_sem=q_recv.at[level, slot],
                device_id=device, device_id_type=MESH)

        def count_send(self, level):
            position = (px, py, pz)[level]
            qr[level, position] = q[...]
            for d in range(1, (NX, NY, NZ)[level]):
                device = along(level, d) if level < 2 else at(z=1 - pz)
                copy = self.copy(level, qr.at[level, position], level * 3 + d - 1, device, position)
                copy.start()
                started.append(copy)

        def count_take(self, level):
            position, size = (px, py, pz)[level], (NX, NY, NZ)[level]
            for d in range(1, size):
                slot = (position + d) % size
                self.copy(level, qr.at[level, slot], level * 3, at(z=1 - pz), slot).wait_recv()
            value = qr[level, 0]
            for i in range(1, size):
                value = value + qr[level, i]
            if level < 2:
                q[...] = value
            else:
                count_ref[...] = value
                inverse = 1.0 / (value + prior_mass)
                for i in range(cents // 128):
                    cb[i * 128:(i + 1) * 128, :] = jnp.transpose(jnp.broadcast_to(inverse[i:i + 1, :], (128, 128)))

        def norm(self, start, size):
            def one(b, carry):
                here = pl.ds(pl.multiple_of(start + b * 128, 128), 128)
                inverse = cb[here, :]
                for j in range(0, width, 128):
                    value = sum_ref[here, j:j + 128] + prior_mass * c_ref[here, j:j + 128].astype(F32)
                    out_ref[here, j:j + 128] = value * inverse
                return carry

            lax.fori_loop(0, size // 128, one, 0)

    stages = [iter(p) for p in programs(Issue(), px, py, pz)]
    for block in ORDER:
        next(stages[block])()
    for copy in soft_out + started:
        copy.wait_send()


def put_out(centroids, counts, log, centroids_out, counts_out, log_out, sem):
    pairs = [(counts, counts_out), (log, log_out)]
    quarter = centroids.shape[0] // 4
    for i in range(4):
        here = slice(i * quarter, (i + 1) * quarter)
        pairs.append((centroids.at[here, :], centroids_out.at[here, :]))
    copies = [pltpu.make_async_copy(a, b, sem.at[i]) for i, (a, b) in enumerate(pairs)]
    for copy in copies:
        copy.start()
    for copy in copies:
        copy.wait()


def body(points, centroids):
    rows, width = points.shape
    cents = centroids.shape[0]
    groups = lax.axis_size("cent")
    found = messages()
    vmem = pl.BlockSpec(memory_space=pltpu.VMEM)
    results = pl.pallas_call(
        functools.partial(kernel, (rows, cents, width, groups)),
        out_shape=(
            pltpu.VMEM((cents, width), F32),
            pltpu.VMEM((cents // 128, 128), F32),
            pltpu.VMEM((8, rows // 8), F32),
        ),
        in_specs=[vmem, pl.BlockSpec(memory_space=pl.ANY)],
        out_specs=(vmem,) * 3,
        scratch_shapes=[
            pltpu.VMEM((cents, width), BF16),
            pltpu.VMEM((cents, width), F32),
            pltpu.VMEM((2, cents, GROUP), F32),
            pltpu.VMEM((width, rows), BF16),
            pltpu.VMEM((rows, width), BF16),
            pltpu.VMEM((cents, rows), BF16),
            pltpu.VMEM((cents, 128), F32),
            pltpu.VMEM((cents, width), F32),
            pltpu.VMEM((found.rows, width), F32),
            pltpu.VMEM((16, rows), BF16),
            pltpu.VMEM((groups, 16, rows // 8), F32),
            pltpu.VMEM((cents // 128, 128), F32),
            pltpu.VMEM((3, 4, cents // 128, 128), F32),
            pltpu.SemaphoreType.DMA((cents // LOAD,)),
            pltpu.SemaphoreType.DMA((groups,)),
            pltpu.SemaphoreType.DMA((groups,)),
            pltpu.SemaphoreType.DMA((9,)),
            pltpu.SemaphoreType.DMA((3, 4)),
            pltpu.SemaphoreType.DMA((len(found.ids),)),
            pltpu.SemaphoreType.DMA((len(found.ids),)),
        ],
        compiler_params=pltpu.CompilerParams(
            collective_id=0, has_side_effects=True, vmem_limit_bytes=56 * 1024 * 1024),
    )(points, centroids)
    new_centroids, counts, log_evidence = pl.pallas_call(
        put_out,
        out_shape=tuple(jax.ShapeDtypeStruct(r.shape, r.dtype) for r in results),
        in_specs=[vmem] * 3,
        out_specs=(pl.BlockSpec(memory_space=pl.ANY),) * 3,
        scratch_shapes=[pltpu.SemaphoreType.DMA((6,))],
        compiler_params=pltpu.CompilerParams(vmem_limit_bytes=1024 * 1024),
    )(*results)
    return new_centroids, counts.reshape(cents), log_evidence.reshape(rows)


def solution(mesh):
    return jax.shard_map(
        body,
        mesh=mesh,
        in_specs=(P("dp", None), P("cent", None)),
        out_specs=(P("cent", None), P("cent"), P("dp")),
        check_vma=False,
    )
```
